256 devices in a mesh: seq: 64 (over z, x_lo, y), head: 4 (over x_hi, core).
Axes of the slice: x: 4 (x_hi: 2, x_lo: 2; x = x_hi * 2 + x_lo), y: 4, z: 8, core: 2. Of those that a mesh axis runs over, the one named last changes fastest.
Arguments:
- queries: bfloat16 [8192, 4096], P('seq', 'head')
- keys: bfloat16 [8192, 1024], P('seq', 'head')
- values: bfloat16 [8192, 1024], P('seq', 'head'), may hold values from -6 to 6
- out_weight: bfloat16 [4096, 4096], P('head'), may hold values from -0.09375 to 0.09375
- windows: int32 [32], replicated, may hold values from 512 to 2048, as said below
- seg_lengths: int32 [64], replicated, may hold values from 1 to 384, 8192 in all
- lang_ids: int32 [64], replicated, may hold values from 0 to 7
Outputs:
- centered: bfloat16 [8192, 4096], P('seq', 'head')
- pooled: float32 [64, 4096], P(None, 'head')
The draws below stay inside these ranges and needn't reach their ends.
Inputs may be any that keep to these rules, and one draw needn't show every extreme that they name: `windows`: each head's window; some head has exactly 2048. `seg_lengths`: the spans tile the document; the longest is exactly 384.
All inputs are finite; a program needn't handle non-finite values.
Results may differ from the reference program's by a relative error of at most 0.014.
Values may be sent and summed in bfloat16 or wider, within the bound.
No kernel may reach another device: no remote copies, remote signals or barrier semaphores. Data moves between devices by JAX's collectives and lax.ppermute only.
A program may use at most 64 MiB of HBM per device.

```python
import math
import jax
import jax.numpy as jnp
import numpy as np
from jax import lax

D = 4096
HEADS = 32
KVH = 8
HD = 128
TOK_DEV = 128
SEGS = 64
NLANG = 8
WINDOW = 2048
LENGTH = 8192
SEG_MOST = 384
N_SEQ = 64


def draw_keys(key, part):
    base = jax.random.normal(jax.random.fold_in(key, 11), (LENGTH, KVH * HD), jnp.float32)
    return base.astype(jnp.bfloat16)


def draw_queries(key, part):
    found = 2.5 * jax.random.normal(jax.random.fold_in(key, 21), (LENGTH, HEADS, HD), jnp.float32)
    return found.reshape(LENGTH, HEADS * HD).astype(jnp.bfloat16)


def draw_windows(key, part):
    spread = jax.random.randint(jax.random.fold_in(key, 31), (HEADS,), WINDOW // 4, WINDOW + 1)
    widest = jax.random.randint(jax.random.fold_in(key, 32), (), 0, HEADS)
    return jnp.where(jnp.arange(HEADS) == widest, WINDOW, spread).astype(jnp.int32)


def set_ends(entries, key, smallest, high):
    shape = entries.shape
    place = [jax.random.randint(jax.random.fold_in(key, axis), (), 0, shape[axis]) for axis in range(len(shape))]
    entries = entries.at[tuple(place)].set(smallest)
    longest = shape.index(max(shape))
    place[longest] = (place[longest] + 1) % shape[longest]
    return entries.at[tuple(place)].set(high)


def shard_levels(own_key, extent, pieces, least, top_value):
    factor_of = 1.0
    for axis_at, parts in pieces:
        heights = jax.random.uniform(jax.random.fold_in(jax.random.fold_in(own_key, 6), axis_at), (parts,), jnp.float32, least / len(pieces), top_value / len(pieces))
        factor_of = factor_of * jnp.repeat(jnp.exp(heights), extent[axis_at] // parts).reshape((-1,) + (1,) * (len(extent) - 1 - axis_at))
    return factor_of


def length_profile(amount, total, bound, skew):
    portions = [(1 << 20) // math.isqrt(standing ** skew) + 1 for standing in range(2, amount + 1)]
    spare, counts = total - bound - (amount - 1), [1] * (amount - 1)
    while spare > 0:
        movable = [i for i in range(amount - 1) if counts[i] < bound]
        whole, remaining = sum([portions[i] for i in movable]), spare
        for i in movable:
            more = min(bound - counts[i], max(1, remaining * portions[i] // whole), spare)
            counts[i] = counts[i] + more
            spare = spare - more
    return np.array([bound] + counts)


def ragged(stream_key, count, total, bound, lean):
    if count == 2:
        one = jax.random.randint(stream_key, (), max(1, total - bound), min(bound, total - 1) + 1)
        return jnp.stack([one, total - one])
    sizes = jnp.asarray(length_profile(count, total, bound, lean), jnp.int32)
    pairs = (count - 1) // 2
    source_of, receiver = sizes[1:1 + 2 * pairs:2], sizes[2:2 + 2 * pairs:2]
    room = jnp.minimum(source_of - 1, bound - receiver)
    shifted = jax.random.randint(jax.random.fold_in(stream_key, 1), (pairs,), 0, 1 << 20) % (room + 1)
    sizes = sizes.at[1:1 + 2 * pairs:2].set(source_of - shifted).at[2:2 + 2 * pairs:2].set(receiver + shifted)
    return sizes[jax.random.permutation(jax.random.fold_in(stream_key, 2), count)]


def scatter_about(stream_key, extent, scale, reach, shards=(), kind=jnp.bfloat16):
    level = shard_levels(stream_key, extent, shards, -0.22, 0.18) if shards else 1.0
    drawn = jax.random.normal(stream_key, extent, jnp.float32) * scale * level
    return jnp.minimum(jnp.maximum(drawn, -reach), reach).astype(kind)


def setup_inputs(seed: int = 0) -> dict:
    key_of = jax.random.split(jax.random.key(seed), 8)
    queries = draw_queries(jax.random.fold_in(key_of[7], 71), 0)
    keys = draw_keys(jax.random.fold_in(key_of[7], 71), 0)
    values = scatter_about(key_of[2], (LENGTH, KVH * HD), 1.0, 6.0, ((0, 64), (1, 4)))
    out_weight = scatter_about(key_of[3], (HEADS * HD, D), (HEADS * HD) ** -0.5, 0.09375, ((0, 4),))
    windows = draw_windows(jax.random.fold_in(key_of[7], 71), 0)
    seg_lengths = ragged(key_of[5], SEGS, LENGTH, SEG_MOST, 2).astype(jnp.int32)
    lang_ids = set_ends(jax.random.randint(key_of[6], (SEGS,), 0, NLANG), jax.random.fold_in(key_of[6], 1), 0, NLANG - 1).astype(jnp.int32)
    return {"queries": queries, "keys": keys, "values": values, "out_weight": out_weight, "windows": windows, "seg_lengths": seg_lengths, "lang_ids": lang_ids}


def reference(queries, keys, values, out_weight, windows, seg_lengths, lang_ids):
    group = HEADS // KVH
    padded_keys = jnp.pad(keys, ((WINDOW, WINDOW), (0, 0)))
    padded_values = jnp.pad(values, ((WINDOW, WINDOW), (0, 0)))
    span = TOK_DEV + 2 * WINDOW
    head_windows = windows.reshape(KVH, group)

    def block(index):
        start = (index * TOK_DEV).astype(jnp.int32)
        query_block = lax.dynamic_slice_in_dim(queries, start, TOK_DEV, 0).astype(jnp.float32).reshape(TOK_DEV, KVH, group, HD)
        key_block = lax.dynamic_slice_in_dim(padded_keys, start, span, 0).astype(jnp.float32).reshape(span, KVH, HD)
        value_block = lax.dynamic_slice_in_dim(padded_values, start, span, 0).astype(jnp.float32).reshape(span, KVH, HD)
        scores = jnp.einsum("tkgd,nkd->kgtn", query_block, key_block) * (HD ** -0.5)
        query_pos = start + jnp.arange(TOK_DEV, dtype=jnp.int32)
        key_pos = start - WINDOW + jnp.arange(span, dtype=jnp.int32)
        distance = jnp.abs(query_pos[:, None] - key_pos[None, :])
        inside = (key_pos >= 0) & (key_pos < LENGTH)
        allowed = (distance[None, None] <= head_windows[:, :, None, None]) & inside[None, None, None, :]
        scores = jnp.where(allowed, scores, jnp.float32(-1e30))
        top = jnp.max(scores, axis=-1, keepdims=True)
        probs = jnp.where(allowed, jnp.exp(scores - top), jnp.float32(0.0))
        denom = jnp.sum(probs, axis=-1)
        rounded = lax.optimization_barrier(probs.astype(jnp.bfloat16)).astype(jnp.float32)
        mixed = jnp.einsum("kgtn,nkd->kgtd", rounded, value_block) / denom[..., None]
        return mixed.transpose(2, 0, 1, 3).reshape(TOK_DEV, HEADS * HD).astype(jnp.bfloat16)

    attn = lax.map(block, jnp.arange(N_SEQ, dtype=jnp.int32)).reshape(LENGTH, HEADS * HD)
    tokens = jnp.dot(attn, out_weight, preferred_element_type=jnp.float32)
    ends = jnp.cumsum(seg_lengths).astype(jnp.int32)
    starts = ends - seg_lengths
    positions = jnp.arange(LENGTH, dtype=jnp.int32)
    seg_hot = ((positions[:, None] >= starts[None, :]) & (positions[:, None] < ends[None, :])).astype(jnp.float32)
    span_sum = jnp.dot(seg_hot.T, tokens, precision=lax.Precision.HIGHEST)
    lang_hot = (lang_ids[:, None] == jnp.arange(NLANG, dtype=jnp.int32)[None, :]).astype(jnp.float32)
    lang_sum = jnp.dot(lang_hot.T, span_sum, precision=lax.Precision.HIGHEST)
    lang_count = jnp.sum(lang_hot * seg_lengths.astype(jnp.float32)[:, None], axis=0)
    lang_mean = lang_sum / jnp.maximum(lang_count, 1.0)[:, None]
    seg_center = jnp.dot(lang_hot, lang_mean, precision=lax.Precision.HIGHEST)
    centered = (tokens - jnp.dot(seg_hot, seg_center, precision=lax.Precision.HIGHEST)).astype(jnp.bfloat16)
    pooled = span_sum / seg_lengths.astype(jnp.float32)[:, None] - seg_center
    return centered, pooled
```

```python
import math

import jax
import jax.numpy as jnp
from jax import lax
from jax.experimental import pallas as pl
from jax.experimental.pallas import tpu as pltpu
from jax.sharding import Mesh, PartitionSpec as P

HD = 128
NLANG = 8
NZ, NXL, NY, NXH, NCORE = 8, 2, 4, 2, 2
PLANE = NXL * NY
TOK = 128
T = PLANE * TOK
REACH = 2048
NK = T + 2 * REACH
SEGS = 64
SPZ = SEGS // NZ
ROWS = TOK + 2 * SPZ
COLS = 1024
NEG = -1e30
EXPC = HD**-0.5 / math.log(2.0)
BQ = 512
BK = 1024


def seg_bounds(lens):
    row = lax.broadcasted_iota(jnp.int32, (SEGS, SEGS), 0)
    col = lax.broadcasted_iota(jnp.int32, (SEGS, SEGS), 1)
    ends = jnp.sum(jnp.where(col <= row, lens, 0.0), axis=1, keepdims=True)
    starts = jnp.sum(jnp.where(col < row, lens, 0.0), axis=1, keepdims=True)
    return starts, ends


def attn_kernel(sc_ref, own_ref, dn_ref, up_ref, a2_ref, len_ref, o_ref, s_ref, kbuf, vbuf, sbuf):
    w = sc_ref[0]
    z = sc_ref[1]
    kbuf[0:T, :] = a2_ref[:, HD : 2 * HD]
    vbuf[0:T, :] = a2_ref[:, 2 * HD : 3 * HD]
    kbuf[T : 2 * T, :] = dn_ref[:, 0:HD]
    vbuf[T : 2 * T, :] = dn_ref[:, HD : 2 * HD]
    kbuf[2 * T : 3 * T, :] = own_ref[:, 0:HD]
    vbuf[2 * T : 3 * T, :] = own_ref[:, HD : 2 * HD]
    kbuf[3 * T : 4 * T, :] = up_ref[:, 0:HD]
    vbuf[3 * T : 4 * T, :] = up_ref[:, HD : 2 * HD]
    kbuf[4 * T : 5 * T, :] = a2_ref[:, 3 * HD : 4 * HD]
    vbuf[4 * T : 5 * T, :] = a2_ref[:, 4 * HD : 5 * HD]
    lo_valid = jnp.maximum(0, REACH - z * T)
    hi_valid = jnp.minimum(NK, REACH + (NZ - z) * T)
    diff = lax.broadcasted_iota(jnp.int32, (BQ, BK), 0) - lax.broadcasted_iota(
        jnp.int32, (BQ, BK), 1
    )

    def qloop(qb, _):
        qs = pl.multiple_of(qb * BQ, BQ)
        q = a2_ref[pl.ds(qs, BQ), 0:HD]
        qf = qs + REACH
        ql = qf + BQ - 1
        lo = jnp.maximum(qf - w, lo_valid)
        hi = jnp.minimum(ql + w + 1, hi_valid)
        b_lo = lo // BK
        b_hi = (hi + BK - 1) // BK
        b_il = jnp.clip((jnp.maximum(ql - w, 0) + BK - 1) // BK, b_lo, b_hi)
        b_ih = jnp.clip((qf + w + 1) // BK, b_il, b_hi)

        def qk(b, mx, masked):
            k0 = pl.multiple_of(b * BK, BK)
            s = lax.dot_general(
                q,
                kbuf[pl.ds(k0, BK), :],
                (((1,), (1,)), ((), ())),
                preferred_element_type=jnp.float32,
            )
            if masked:
                s = jnp.where(jnp.abs(diff + (qf - k0)) <= w, s, NEG)
            sbuf[b] = s
            for c in range(BK // 128):
                mx = jnp.maximum(mx, s[:, c * 128 : (c + 1) * 128])
            return mx

        mx = jnp.full((BQ, 128), NEG, jnp.float32)
        mx = lax.fori_loop(b_lo, b_il, lambda b, c: qk(b, c, True), mx)
        mx = lax.fori_loop(b_il, b_ih, lambda b, c: qk(b, c, False), mx)
        mx = lax.fori_loop(b_ih, b_hi, lambda b, c: qk(b, c, True), mx)
        m = jnp.max(mx, axis=1, keepdims=True)

        def pv(b, carry):
            total, acc = carry
            k0 = pl.multiple_of(b * BK, BK)
            p = jnp.exp2((sbuf[b] - m) * EXPC)
            for c in range(BK // 128):
                total = total + p[:, c * 128 : (c + 1) * 128]
            acc = acc + lax.dot_general(
                p.astype(jnp.bfloat16),
                vbuf[pl.ds(k0, BK), :],
                (((1,), (0,)), ((), ())),
                preferred_element_type=jnp.float32,
            )
            return total, acc

        total, acc = lax.fori_loop(
            b_lo,
            b_hi,
            pv,
            (jnp.zeros((BQ, 128), jnp.float32), jnp.zeros((BQ, HD), jnp.float32)),
        )
        denom = jnp.sum(total, axis=1, keepdims=True)
        o_ref[pl.ds(qs, BQ), :] = (acc / denom).astype(jnp.bfloat16)
        return 0

    lax.fori_loop(0, T // BQ, qloop, 0)
    starts, ends = seg_bounds(len_ref[...].astype(jnp.float32))
    pos = (lax.broadcasted_iota(jnp.int32, (SEGS, T), 1) + z * T).astype(jnp.float32)
    hot = jnp.where((pos >= starts) & (pos < ends), 1.0, 0.0).astype(jnp.bfloat16)
    s_ref[...] = jnp.dot(hot, o_ref[...], preferred_element_type=jnp.float32)


def attention(scalars, own, down, up, mixed, lens_row):
    vmem = pl.BlockSpec(memory_space=pltpu.VMEM)
    return pl.pallas_call(
        attn_kernel,
        out_shape=(
            jax.ShapeDtypeStruct((T, HD), jnp.bfloat16),
            jax.ShapeDtypeStruct((SEGS, HD), jnp.float32),
        ),
        in_specs=[pl.BlockSpec(memory_space=pltpu.SMEM), vmem, vmem, vmem, vmem, vmem],
        out_specs=(vmem, vmem),
        scratch_shapes=[
            pltpu.VMEM((NK, HD), jnp.bfloat16),
            pltpu.VMEM((NK, HD), jnp.bfloat16),
            pltpu.VMEM((NK // BK, BQ, BK), jnp.float32),
        ],
        name="window_attention",
    )(scalars, own, down, up, mixed, lens_row)


def proj_kernel(x_ref, w_ref, o_ref):
    acc = jnp.zeros((ROWS, COLS), jnp.float32)
    for r in range(PLANE):
        acc = acc + jnp.dot(
            x_ref[r], w_ref[r * HD : (r + 1) * HD, :], preferred_element_type=jnp.float32
        )
    hi, lo = split_rows(acc[TOK : TOK + SPZ] + acc[TOK + SPZ :])
    o_ref[0, 0, 0:TOK, :] = acc[0:TOK].astype(jnp.bfloat16)
    o_ref[0, 0, TOK:ROWS, :] = jnp.concatenate([hi, lo], axis=0).astype(jnp.bfloat16)


def split_rows(x):
    hi = x.astype(jnp.bfloat16).astype(jnp.float32)
    return hi, x - hi


def project(x, out_weight):
    return pl.pallas_call(
        proj_kernel,
        grid=(NXH * NCORE,),
        out_shape=jax.ShapeDtypeStruct((NCORE, NXH, ROWS, COLS), jnp.bfloat16),
        in_specs=[
            pl.BlockSpec((PLANE, ROWS, HD), lambda j: (0, 0, 0)),
            pl.BlockSpec((PLANE * HD, COLS), lambda j: (0, j)),
        ],
        out_specs=pl.BlockSpec((1, 1, ROWS, COLS), lambda j: (j % NCORE, j // NCORE, 0, 0)),
        name="projection",
    )(x, out_weight)


def merge_kernel(y_ref, o_ref):
    acc = y_ref[0, 0].astype(jnp.float32) + y_ref[1, 0].astype(jnp.float32)
    hi, lo = split_rows(acc[TOK : TOK + SPZ] + acc[TOK + SPZ :])
    o_ref[0, 0:TOK, :] = acc[0:TOK].astype(jnp.bfloat16)
    o_ref[0, TOK:ROWS, :] = jnp.concatenate([hi, lo], axis=0).astype(jnp.bfloat16)


def merge(y):
    return pl.pallas_call(
        merge_kernel,
        grid=(NXH,),
        out_shape=jax.ShapeDtypeStruct((NXH, ROWS, COLS), jnp.bfloat16),
        in_specs=[pl.BlockSpec((NCORE, 1, ROWS, COLS), lambda j: (0, j, 0, 0))],
        out_specs=pl.BlockSpec((1, ROWS, COLS), lambda j: (j, 0, 0)),
        name="merge",
    )(y)


def final_kernel(sc_ref, y_ref, span_ref, len_ref, lenc_ref, idr_ref, idc_ref, c_ref, p_ref):
    base = sc_ref[2]
    lens = len_ref[...].astype(jnp.float32)
    starts, ends = seg_bounds(lens)
    pos = (lax.broadcasted_iota(jnp.int32, (SEGS, TOK), 1) + base).astype(jnp.float32)
    hot = jnp.where((pos >= starts) & (pos < ends), 1.0, 0.0)
    same = jnp.where(idc_ref[...] == idr_ref[...], 1.0, 0.0)
    count = jnp.maximum(jnp.sum(same * lens, axis=1, keepdims=True), 1.0)
    spans = span_ref[...]
    center = (
        jnp.dot(
            same, spans, precision=lax.Precision.HIGHEST, preferred_element_type=jnp.float32
        )
        / count
    )
    p_ref[...] = spans / lenc_ref[...].astype(jnp.float32) - center
    tokens = y_ref[0, 0:TOK, :].astype(jnp.float32) + y_ref[1, 0:TOK, :].astype(jnp.float32)
    mean = lax.dot_general(
        hot,
        center,
        (((0,), (0,)), ((), ())),
        precision=lax.Precision.HIGHEST,
        preferred_element_type=jnp.float32,
    )
    c_ref[...] = (tokens - mean).astype(jnp.bfloat16)


def finalize(scalars, y, spans, seg_lengths, lang_ids):
    vmem = pl.BlockSpec(memory_space=pltpu.VMEM)
    return pl.pallas_call(
        final_kernel,
        out_shape=(
            jax.ShapeDtypeStruct((TOK, COLS), jnp.bfloat16),
            jax.ShapeDtypeStruct((SEGS, COLS), jnp.float32),
        ),
        in_specs=[pl.BlockSpec(memory_space=pltpu.SMEM)] + [vmem] * 6,
        out_specs=(vmem, vmem),
        name="centre",
    )(
        scalars,
        y,
        spans,
        seg_lengths.reshape(1, SEGS),
        seg_lengths.reshape(SEGS, 1),
        lang_ids.reshape(1, SEGS),
        lang_ids.reshape(SEGS, 1),
    )


def shifted(block, axis, distance):
    devices = range(lax.axis_size(axis))
    route = [(i - distance, i) for i in devices if i - distance in devices]
    return lax.ppermute(block, axis, route)


def exchange(x, axes):
    return lax.all_to_all(x, axes, 0, 0, tiled=True)


def on_device(queries, keys, values, out_weight, windows, seg_lengths, lang_ids):
    plane_axes = ("xl", "y")
    z = lax.axis_index("z")
    rank = lax.axis_index("xl") * NY + lax.axis_index("y")
    head = (lax.axis_index("xh") * NCORE + lax.axis_index("core")) * PLANE + rank
    window = lax.dynamic_index_in_dim(windows, head, keepdims=False)
    scalars = jnp.stack([window, z, (z * PLANE + rank) * TOK]).astype(jnp.int32)
    raw = jnp.stack(
        [
            jnp.concatenate([keys[:, j * HD : (j + 1) * HD], values[:, j * HD : (j + 1) * HD]], 1)
            for j in range(2)
        ]
    )
    far_down = shifted(raw, "z", 2)
    far_up = shifted(raw, "z", -2)
    own = exchange(jnp.repeat(raw, PLANE // 2, axis=0), plane_axes).reshape(T, 2 * HD)
    down = shifted(own, "z", 1)
    up = shifted(own, "z", -1)
    by_head = queries.reshape(TOK, PLANE, HD).transpose(1, 0, 2)
    mixed = jnp.concatenate(
        [by_head, jnp.repeat(far_down, PLANE // 2, axis=0), jnp.repeat(far_up, PLANE // 2, axis=0)],
        axis=2,
    )
    mixed = exchange(mixed, plane_axes).reshape(T, 5 * HD)
    attn, span_attn = attention(scalars, own, down, up, mixed, seg_lengths.reshape(1, SEGS))
    span_mine = jnp.sum(exchange(span_attn.reshape(NZ, SPZ, HD), "z"), axis=0)
    hi, lo = split_rows(span_mine)
    span_rows = jnp.concatenate([hi, lo], axis=0).astype(jnp.bfloat16)
    x = jnp.concatenate(
        [attn.reshape(PLANE, TOK, HD), jnp.broadcast_to(span_rows, (PLANE, 2 * SPZ, HD))], axis=1
    )
    x = exchange(x, plane_axes)
    y = merge(exchange(project(x, out_weight), "core"))
    y = exchange(y, "xh")
    span_mine = jnp.sum(y[:, TOK:].astype(jnp.float32).reshape(2 * NXH, SPZ, COLS), axis=0)
    spans = exchange(
        jnp.broadcast_to(span_mine, (NZ, SPZ, COLS)), "z"
    ).reshape(SEGS, COLS)
    return finalize(scalars, y, spans, seg_lengths, lang_ids)


def solution(mesh):
    split = Mesh(
        mesh.devices.reshape(NZ, NXL, NY, NXH, NCORE), ("z", "xl", "y", "xh", "core")
    )
    seq = ("z", "xl", "y")
    head = ("xh", "core")
    in_specs = (
        P(seq, head),
        P(seq, head),
        P(seq, head),
        P(head, None),
        P(),
        P(),
        P(),
    )
    out_specs = (P(seq, head), P(None, head))
    return jax.shard_map(
        on_device, mesh=split, in_specs=in_specs, out_specs=out_specs, check_vma=False
    )
```
